512 devices in a mesh: wide: 128 (over y_hi, x, z), narrow: 4 (over y_lo, core).
Axes of the slice: x: 4, y: 8 (y_hi: 4, y_lo: 2; y = y_hi * 2 + y_lo), z: 8, core: 2. Of those that a mesh axis runs over, the one named last changes fastest.
Arguments:
- tokens: bfloat16 [16384, 1024], P('wide'), may hold values from -6 to 6
- cotangent: bfloat16 [16384, 1024], P('wide'), may hold values from -6 to 6
- expert_ids: int32 [16384, 1], P('wide'), may hold values from 0 to 31; in each aligned block of 128 rows (0 to 127, 128 to 255, ...) at most 16 rows name the same one
- route_prob: float32 [16384], P('wide'), may hold values from 0.2 to 1
- gate_weight: bfloat16 [32768, 2816], P('wide', 'narrow'), may hold values from -0.1875 to 0.1875
- up_weight: bfloat16 [32768, 2816], P('wide', 'narrow'), may hold values from -0.1875 to 0.1875
- down_weight: bfloat16 [32768, 2816], P('wide', 'narrow'), may hold values from -0.109375 to 0.109375
Outputs:
- output: bfloat16 [16384, 1024], P('wide', 'narrow')
- tokens_grad: bfloat16 [16384, 1024], P('wide', 'narrow')
- prob_grad: float32 [16384], P('wide')
- gate_grad: float32 [32768, 2816], P('wide', 'narrow')
- up_grad: float32 [32768, 2816], P('wide', 'narrow')
- down_grad: float32 [32768, 2816], P('wide', 'narrow')
The draws below stay inside these ranges and needn't reach their ends.
Inputs may be any that keep to these rules, and one draw needn't show every extreme that they name: `expert_ids`: among the 128 tokens of one index of wide, no expert is chosen by more than 16 tokens, and in some such groups one expert is chosen by exactly 16.
All inputs are finite; a program needn't handle non-finite values.
Results may differ from the reference program's by a relative error of at most 0.01.
Values may be sent and summed in bfloat16 or wider, within the bound.
A program may use at most 64 MiB of HBM per device.

```python
import math
import jax
import jax.numpy as jnp
import numpy as np
from jax import lax

D = 1024
FF = 2816
TOK_DEV = 128
EXPERTS = 32
CAP = 16
TOKENS = 16384
N_NARROW = 4


def level_of(rng, dims, split, low, top_value):
    level = 1.0
    for dim, parts in split:
        draws = jax.random.uniform(jax.random.fold_in(jax.random.fold_in(rng, 6), dim), (parts,), jnp.float32, low / len(split), top_value / len(split))
        level = level * jnp.repeat(jnp.exp(draws), dims[dim] // parts).reshape((-1,) + (1,) * (len(dims) - 1 - dim))
    return level


def shared_out(key, own, number, rows, number_of, top, limit, lean):
    sequence = jax.random.permutation(key, number_of)
    packed, common = portions_of(number_of, rows * top, limit, lean, True), portions_of(number_of, rows * top, limit, lean, False)
    places = jnp.arange(number_of)

    def named(lengths, rotation):
        used = int((lengths > 0).sum())
        fixed = max(1, used // 4)
        shifted = fixed + (places - fixed + rotation * (used - fixed)) % max(1, number_of - fixed)
        return jnp.zeros((number_of,), jnp.int32).at[sequence[jnp.where(places < fixed, places, shifted)]].set(jnp.asarray(lengths, jnp.int32))

    lengths = jnp.where(number % 4 == 0, named(packed, number // 4), named(common, number - number // 4 - 1))
    mixed = jax.random.permutation(jax.random.fold_in(own, 3), number_of)
    source_of, receiver = mixed[0:number_of // 2 * 2:2], mixed[1:number_of // 2 * 2:2]
    slack = jnp.minimum(lengths[source_of] - 1, limit - lengths[receiver]) // 2
    slack = jnp.where((source_of == sequence[0]) | (receiver == sequence[0]) | (lengths[receiver] == 0), 0, jnp.maximum(slack, 0))
    shifted = jax.random.randint(jax.random.fold_in(own, 4), (number_of // 2,), 0, 1 << 20) % (slack + 1)
    lengths = lengths.at[source_of].add(-shifted).at[receiver].add(shifted)
    labels = jnp.searchsorted(jnp.cumsum(lengths), jnp.arange(rows * top), side="right").astype(jnp.int32)
    table = labels.reshape(top, rows).T
    table = table[jax.random.permutation(jax.random.fold_in(own, 1), rows)]
    rotation = jax.random.randint(jax.random.fold_in(own, 2), (rows, 1), 0, top)
    return jnp.take_along_axis(table, (jnp.arange(top)[None, :] + rotation) % top, axis=1)


def portions_of(amount, total, limit, lean, full):
    weights = [(1 << 20) // math.isqrt(rank ** lean) + 1 for rank in range(1, amount + 1)]
    largest = limit if full else min(limit, max(-(-total // amount), total * weights[0] // sum(weights)))
    least = 1 if total - largest >= amount - 1 else 0
    given, spare = [largest] + [least] * (amount - 1), total - largest - least * (amount - 1)
    while spare > 0:
        candidates = [i for i in range(1, amount) if given[i] < largest] or [i for i in range(1, amount) if given[i] < limit]
        mass, budget = sum([weights[i] for i in candidates]), spare
        for i in candidates:
            extra = min(limit - given[i], max(1, budget * weights[i] // mass), spare)
            given[i] = given[i] + extra
            spare = spare - extra
    return np.array(given)


def bell_draw(stream_key, dims, width, most, shards=(), kind=jnp.bfloat16):
    factor_of = level_of(stream_key, dims, shards, -0.22, 0.18) if shards else 1.0
    entries = jax.random.normal(stream_key, dims, jnp.float32) * width * factor_of
    return jnp.minimum(jnp.maximum(entries, -most), most).astype(kind)


def setup_inputs(seed: int = 0) -> dict:
    splits = jax.random.split(jax.random.key(seed), 8)
    tokens = bell_draw(splits[0], (TOKENS, D), 1.0, 6.0, ((0, 128),))
    cotangent = bell_draw(splits[1], (TOKENS, D), 1.0, 6.0, ((0, 128),))
    expert_ids_keys = jax.random.split(jax.random.fold_in(splits[2], 1), TOKENS // TOK_DEV)
    expert_ids_turns = jax.random.permutation(jax.random.fold_in(splits[2], 3), TOKENS // TOK_DEV)
    expert_ids = jax.vmap(lambda own, number: shared_out(jax.random.fold_in(splits[2], 2), own, number, TOK_DEV, EXPERTS, 1, CAP, 2))(expert_ids_keys, expert_ids_turns).reshape((TOKENS, 1))
    route_prob = jnp.clip(0.2 + 0.8 * jax.random.uniform(splits[3], (TOKENS,), jnp.float32) ** level_of(splits[3], (TOKENS,), ((0, 128),), -0.2, 0.2), 0.2, 1.0)
    gate_weight = bell_draw(splits[4], (EXPERTS * D, FF), D ** -0.5, 0.1875, ((0, 128), (1, 4)))
    up_weight = bell_draw(splits[5], (EXPERTS * D, FF), D ** -0.5, 0.1875, ((0, 128), (1, 4)))
    down_weight = bell_draw(splits[6], (EXPERTS * D, FF), FF ** -0.5, 0.109375, ((0, 128), (1, 4)))
    return dict(tokens=tokens, cotangent=cotangent, expert_ids=expert_ids, route_prob=route_prob, gate_weight=gate_weight, up_weight=up_weight, down_weight=down_weight)


def rounded_term(value):
    return lax.optimization_barrier(value.astype(jnp.bfloat16)).astype(jnp.float32)


def reference(tokens, cotangent, expert_ids, route_prob, gate_weight, up_weight, down_weight):
    block_rows = 128
    block_total = TOKENS // block_rows + EXPERTS
    padded_rows = block_total * block_rows
    fourth = FF // N_NARROW
    chosen = expert_ids[:, 0].astype(jnp.int32)
    sorted_order = jnp.argsort(chosen, stable=True).astype(jnp.int32)
    counts = jnp.sum((chosen[:, None] == jnp.arange(EXPERTS, dtype=jnp.int32)[None, :]).astype(jnp.int32), axis=0)
    starts = jnp.cumsum(counts) - counts
    rounded = (counts + block_rows - 1) // block_rows * block_rows
    offsets = jnp.cumsum(rounded) - rounded
    sorted_ids = chosen[sorted_order]
    slot_sorted = (offsets[sorted_ids] + jnp.arange(TOKENS, dtype=jnp.int32) - starts[sorted_ids]).astype(jnp.int32)
    source = jnp.full((padded_rows,), TOKENS, jnp.int32).at[slot_sorted].set(sorted_order)
    slot_token = jnp.zeros((TOKENS,), jnp.int32).at[sorted_order].set(slot_sorted)
    block_start = jnp.arange(block_total, dtype=jnp.int32) * block_rows
    block_expert = jnp.minimum(jnp.sum(((offsets + rounded)[None, :] <= block_start[:, None]).astype(jnp.int32), axis=1), EXPERTS - 1).astype(jnp.int32)
    scaled = (route_prob[:, None] * cotangent.astype(jnp.float32)).astype(jnp.bfloat16)
    blank_row = jnp.zeros((1, D), jnp.bfloat16)
    padded_in = jnp.concatenate([tokens, blank_row], 0)
    padded_cot = jnp.concatenate([scaled, blank_row], 0)
    gate_all = gate_weight.reshape(EXPERTS, D, FF)
    up_all = up_weight.reshape(EXPERTS, D, FF)
    down_all = down_weight.reshape(EXPERTS, D, FF)

    def block_step(state_tuple, block_index):
        gate_acc, up_acc, down_acc = state_tuple
        expert = block_expert[block_index]
        picks = lax.dynamic_slice_in_dim(source, block_index * block_rows, block_rows)
        rows_in = padded_in[picks]
        rows_cot = padded_cot[picks]
        gate_mat = gate_all[expert]
        up_mat = up_all[expert]
        down_mat = down_all[expert]
        gate_val = jnp.dot(rows_in, gate_mat, preferred_element_type=jnp.float32)
        up_val = jnp.dot(rows_in, up_mat, preferred_element_type=jnp.float32)
        gate_sigma = jax.nn.sigmoid(gate_val)
        active = gate_val * gate_sigma
        hidden = (active * up_val).astype(jnp.bfloat16)
        d_hidden = jnp.dot(rows_cot, down_mat, preferred_element_type=jnp.float32)
        d_gate = (d_hidden * up_val * gate_sigma * (1.0 + gate_val * (1.0 - gate_sigma))).astype(jnp.bfloat16)
        d_up = (d_hidden * active).astype(jnp.bfloat16)
        ffn_sum = jnp.zeros((block_rows, D), jnp.float32)
        grad_sum = jnp.zeros((block_rows, D), jnp.float32)
        for quarter in range(N_NARROW):
            low = quarter * fourth
            high = low + fourth
            ffn_sum = ffn_sum + rounded_term(jnp.dot(hidden[:, low:high], down_mat[:, low:high].T, preferred_element_type=jnp.float32))
            term = jnp.dot(d_gate[:, low:high], gate_mat[:, low:high].T, preferred_element_type=jnp.float32)
            term = term + jnp.dot(d_up[:, low:high], up_mat[:, low:high].T, preferred_element_type=jnp.float32)
            grad_sum = grad_sum + rounded_term(term)
        gate_acc = gate_acc.at[expert].add(jnp.dot(rows_in.T, d_gate, preferred_element_type=jnp.float32))
        up_acc = up_acc.at[expert].add(jnp.dot(rows_in.T, d_up, preferred_element_type=jnp.float32))
        down_acc = down_acc.at[expert].add(jnp.dot(rows_cot.T, hidden, preferred_element_type=jnp.float32))
        return (gate_acc, up_acc, down_acc), (ffn_sum.astype(jnp.bfloat16), grad_sum.astype(jnp.bfloat16))

    zero_grads = jnp.zeros((EXPERTS, D, FF), jnp.float32)
    state_tuple, outputs = lax.scan(block_step, (zero_grads, zero_grads, zero_grads), jnp.arange(block_total, dtype=jnp.int32))
    ffn_rows = outputs[0].reshape(padded_rows, D)[slot_token]
    grad_rows = outputs[1].reshape(padded_rows, D)[slot_token]
    output = (route_prob[:, None] * ffn_rows.astype(jnp.float32)).astype(jnp.bfloat16)
    prob_grad = jnp.sum(ffn_rows.astype(jnp.float32) * cotangent.astype(jnp.float32), axis=1)
    gate_grad = state_tuple[0].reshape(EXPERTS * D, FF)
    up_grad = state_tuple[1].reshape(EXPERTS * D, FF)
    down_grad = state_tuple[2].reshape(EXPERTS * D, FF)
    return (output, grad_rows, prob_grad, gate_grad, up_grad, down_grad)
```

```python
import functools

import jax
import jax.numpy as jnp
from jax import lax
from jax.experimental import pallas as pl
from jax.experimental.pallas import tpu as pltpu
from jax.sharding import PartitionSpec as P

CAP = 16
CHUNK = 256
F32 = jnp.float32
BF16 = jnp.bfloat16


def dot(a, b):
    return lax.dot_general(a, b, (((1,), (0,)), ((), ())), preferred_element_type=F32)


def dot_t(a, b):
    return lax.dot_general(a, b, (((1,), (1,)), ((), ())), preferred_element_type=F32)


def kernel(
    tok, cot, ids, prob, wg, wu, wd,
    o_out, o_grad, o_prob, o_gg, o_gu, o_gd,
    wall, sendbuf, x4, xt, pre, act3, out_acc, in_acc, gloc, r_right, r_left, stage,
    t1s, t1r, t2s, t2r, fo, back, place, probs, parts,
    ag_send, ag_recv, rs_send, rs_recv, a_send, a_recv, l_sem, n_send, n_recv,
    t1_send, t1_recv, t2_send, t2_recv, b_send, b_recv, p_send, p_recv,
):
    toks, width = tok.shape
    ff = wg.shape[1]
    nf, _, _, quarter, chunk = wall.shape
    experts = sendbuf.shape[0] // CAP
    rows = x4.shape[1]
    blocks = rows // CAP
    me = lax.axis_index("wide")
    n = lax.axis_index("narrow")
    m = lax.rem(me, 4)
    e0 = lax.div(me, 4)
    half = lax.rem(e0, 2)
    group = lax.div(me, 8)
    i0 = group * 2
    core_peer = n + 1 - 2 * lax.rem(n, 2)
    row_peer = lax.rem(n + 2, 4)
    far_peer = 3 - n

    def dest_of(e):
        h = lax.rem(e + half, 2)
        return 4 * e + m + h * (3 - 2 * m), i0 + h

    def source_of(i):
        h = lax.rem(i, 2)
        return lax.div(i, 2) * 8 + lax.rem(half + h, 2) * 4 + m + h * (3 - 2 * m)

    def remote(src, dst, ssem, rsem, wide, narrow):
        return pltpu.make_async_remote_copy(
            src_ref=src, dst_ref=dst, send_sem=ssem, recv_sem=rsem,
            device_id={"wide": wide, "narrow": narrow}, device_id_type=pl.DeviceIdType.MESH,
        )

    def await_bytes(ref, sem):
        pltpu.make_async_copy(ref, ref, sem).wait()

    for f in range(nf):
        w = min(chunk, ff - f * chunk)
        for k, ref in enumerate((wg, wu, wd)):
            part = ref[:, f * chunk : f * chunk + w]
            if w < chunk:
                part = jnp.concatenate([part, jnp.zeros((quarter, chunk - w), BF16)], axis=1)
            wall[f, m, k] = part

    barrier = pltpu.get_barrier_semaphore()

    def signal(wide, narrow):
        pl.semaphore_signal(
            barrier, inc=1, device_id={"wide": wide, "narrow": narrow},
            device_id_type=pl.DeviceIdType.MESH,
        )

    for turn in (1, 3):
        signal(4 * e0 + lax.rem(m + turn, 4), n)

    for peer in (core_peer, row_peer, far_peer):
        signal(me, peer)

    @pl.loop(1, experts)
    def _(j):
        signal(dest_of(lax.rem(e0 + j, experts))[0], n)

    @pl.loop(1, blocks)
    def _(j):
        signal(source_of(lax.rem(i0 + j, blocks)), n)

    def iota(shape, axis):
        return lax.broadcasted_iota(jnp.int32, shape, axis).astype(F32)

    slots = experts * CAP
    idf = ids[...].astype(F32)
    onehot = jnp.where(iota((toks, experts), 1) == idf, 1.0, 0.0)
    row_i, col_i = iota((toks, toks), 0), iota((toks, toks), 1)
    lower = jnp.where(col_i < row_i, 1.0, 0.0).astype(BF16)
    rank = jnp.sum(dot(lower, onehot.astype(BF16)) * onehot, axis=1, keepdims=True)
    slot = idf * CAP + rank
    place[...] = jnp.where(iota((toks, slots), 1) == slot, 1.0, 0.0).astype(BF16)
    diag = row_i == col_i
    slot_row = jnp.sum(jnp.where(diag, slot, 0.0), axis=0, keepdims=True)
    prob_col = jnp.sum(jnp.where(diag, prob[...], 0.0), axis=1, keepdims=True)
    probs[...] = jnp.broadcast_to(prob_col, (toks, quarter))
    columns = pl.ds(pl.multiple_of(n * quarter, quarter), quarter)
    pick = jnp.where(iota((slots, toks), 0) == slot_row, 1.0, 0.0).astype(BF16)
    scaled = (prob_col * cot[:, columns].astype(F32)).astype(BF16)
    sendbuf[:, :quarter] = dot(pick, tok[:, columns]).astype(BF16)
    sendbuf[:, quarter:] = dot(pick, scaled).astype(BF16)

    pl.semaphore_wait(barrier, experts - 1 + blocks - 1 + 5)

    def rows_at(i):
        return pl.ds(pl.multiple_of(i * CAP, CAP), CAP)

    local_in = pltpu.make_async_copy(
        sendbuf.at[rows_at(e0)], x4.at[n, rows_at(i0)], l_sem.at[0]
    )
    local_in.start()

    @pl.loop(1, experts)
    def _(j):
        e = lax.rem(e0 + j, experts)
        wide, block = dest_of(e)
        remote(sendbuf.at[rows_at(e)], x4.at[n, rows_at(block)], a_send, a_recv, wide, n).start()

    def ag_right(f, q):
        return remote(
            wall.at[f, q], wall.at[f, q], ag_send.at[0, f, q], ag_recv.at[f, q], me + 1, n
        )

    def ag_left(f, q):
        return remote(
            wall.at[f, q], wall.at[f, q], ag_send.at[1, f, q], ag_recv.at[f, q], me - 1, n
        )

    def ag_own(f):
        @pl.when(m < 3)
        def _():
            ag_right(f, m).start()

        @pl.when(m > 0)
        def _():
            ag_left(f, m).start()

    def ag_step(f, d):
        @pl.when(m >= d)
        def _():
            await_bytes(wall.at[f, m - d], ag_recv.at[f, m - d])

            @pl.when(m < 3)
            def _():
                ag_right(f, m - d).start()

        @pl.when(m + d <= 3)
        def _():
            await_bytes(wall.at[f, m + d], ag_recv.at[f, m + d])

            @pl.when(m > 0)
            def _():
                ag_left(f, m + d).start()

    ag_own(0)
    ag_step(0, 1)
    local_in.wait()
    await_bytes(x4.at[n, pl.ds(0, rows - CAP)], a_recv)
    to_row = remote(x4.at[n], x4.at[n], n_send.at[1], n_recv.at[n], me, row_peer)
    to_core = remote(x4.at[n], x4.at[n], n_send.at[0], n_recv.at[n], me, core_peer)
    to_row.start()
    to_core.start()
    out_acc[...] = jnp.zeros_like(out_acc)
    in_acc[...] = jnp.zeros_like(in_acc)
    ag_step(0, 2)
    await_bytes(x4.at[row_peer], n_recv.at[row_peer])
    relay = remote(x4.at[row_peer], x4.at[row_peer], n_send.at[2], n_recv.at[row_peer], me, core_peer)
    relay.start()
    ag_step(0, 3)
    ag_own(1)
    await_bytes(x4.at[core_peer], n_recv.at[core_peer])
    await_bytes(x4.at[far_peer], n_recv.at[far_peer])

    eye = jnp.where(iota((quarter, quarter), 0) == iota((quarter, quarter), 1), 1.0, 0.0).astype(BF16)

    @pl.loop(0, 4)
    def _(q):
        for k in range(2):
            part = pl.ds(k * quarter, quarter)
            xt[q, part, :] = dot_t(eye, x4[q, :, part]).astype(BF16)

    def rs_right(f, q):
        return remote(
            stage.at[f, q], r_right.at[f, q], rs_send.at[f, q], rs_recv.at[0, f, q], me + 1, n
        )

    def rs_left(f, q):
        return remote(
            stage.at[f, q], r_left.at[f, q], rs_send.at[f, q], rs_recv.at[1, f, q], me - 1, n
        )

    def rs_first(f):
        @pl.when(m == 0)
        def _():
            for q in (3, 2, 1):
                stage[f, q] = gloc[f, q].astype(BF16)
                rs_right(f, q).start()

        @pl.when(m == 3)
        def _():
            for q in (0, 1, 2):
                stage[f, q] = gloc[f, q].astype(BF16)
                rs_left(f, q).start()

    def rs_relay(f):
        for q, p in ((3, 0), (2, 1)):
            @pl.when((m > 0) & (m < q))
            def _():
                await_bytes(r_right.at[f, q], rs_recv.at[0, f, q])
                stage[f, q] = (gloc[f, q] + r_right[f, q].astype(F32)).astype(BF16)
                rs_right(f, q).start()

            @pl.when((m < 3) & (m > p))
            def _():
                await_bytes(r_left.at[f, p], rs_recv.at[1, f, p])
                stage[f, p] = (gloc[f, p] + r_left[f, p].astype(F32)).astype(BF16)
                rs_left(f, p).start()

    step_rows = min(64, rows)

    @pl.loop(0, nf)
    def _(f):
        for k, first, source in ((0, 0, 0), (1, 0, 1), (2, quarter, 2)):
            total = dot(x4[0, :, first : first + quarter], wall[f, 0, source])
            for q in range(1, 4):
                total += dot(x4[q, :, first : first + quarter], wall[f, q, source])
            pre[k] = total

        @pl.loop(0, rows // step_rows)
        def _(r):
            part = pl.ds(pl.multiple_of(r * step_rows, step_rows), step_rows)
            gate, up, d_hidden = pre[0, part], pre[1, part], pre[2, part]
            sigma = jax.nn.sigmoid(gate)
            active = gate * sigma
            act3[0, part] = (active * up).astype(BF16)
            act3[1, part] = (d_hidden * up * sigma * (1.0 + gate * (1.0 - sigma))).astype(BF16)
            act3[2, part] = (d_hidden * active).astype(BF16)

        @pl.loop(0, 4)
        def _(q):
            gloc[f, q, 0] = dot(xt[q, :quarter], act3[1])
            gloc[f, q, 1] = dot(xt[q, :quarter], act3[2])
            gloc[f, q, 2] = dot(xt[q, quarter:], act3[0])

        rs_first(f)

        @pl.loop(0, 4)
        def _(q):
            out_acc[q] += dot_t(act3[0], wall[f, q, 2])
            in_acc[q] += dot_t(act3[1], wall[f, q, 0]) + dot_t(act3[2], wall[f, q, 1])

        @pl.when(f + 1 < nf)
        def _():
            for d in (1, 2, 3):
                ag_step(f + 1, d)

            @pl.when(f + 2 < nf)
            def _():
                ag_own(f + 2)

        @pl.when(f >= 1)
        def _():
            rs_relay(f - 1)

    def both(q):
        return jnp.concatenate([out_acc[q], in_acc[q]], axis=1)

    t1s[1] = both(far_peer).astype(BF16)
    t1_far = remote(t1s.at[1], t1r.at[1], t1_send.at[1], t1_recv.at[1], me, core_peer)
    t1_far.start()
    t1s[0] = both(core_peer).astype(BF16)
    t1_near = remote(t1s.at[0], t1r.at[0], t1_send.at[0], t1_recv.at[0], me, core_peer)
    t1_near.start()
    t1_far.wait_recv()
    t2s[...] = (both(row_peer) + t1r[1].astype(F32)).astype(BF16)
    t2 = remote(t2s, t2r, t2_send, t2_recv, me, row_peer)
    t2.start()
    t1_near.wait_recv()
    t2.wait_recv()
    fo[...] = (both(n) + t1r[0].astype(F32) + t2r[...].astype(F32)).astype(BF16)

    local_back = pltpu.make_async_copy(fo.at[rows_at(i0)], back.at[rows_at(e0)], l_sem.at[1])
    local_back.start()

    @pl.loop(1, blocks)
    def _(j):
        i = lax.rem(i0 + j, blocks)
        remote(fo.at[rows_at(i)], back.at[rows_at(e0)], b_send, b_recv, source_of(i), n).start()

    rs_relay(nf - 1)

    def finish(f):
        w = min(chunk, ff - f * chunk)

        @pl.when(m > 0)
        def _():
            await_bytes(r_right.at[f, m], rs_recv.at[0, f, m])
            gloc[f, m] += r_right[f, m].astype(F32)

        @pl.when(m < 3)
        def _():
            await_bytes(r_left.at[f, m], rs_recv.at[1, f, m])
            gloc[f, m] += r_left[f, m].astype(F32)

        for k, ref in enumerate((o_gg, o_gu, o_gd)):
            ref[:, f * chunk : f * chunk + w] = gloc[f, m, k][:, :w]

    for f in range(nf - 1):
        finish(f)

    local_back.wait()
    await_bytes(back.at[pl.ds(0, slots - CAP)], b_recv)
    ffn = dot(place[...], back[:, :quarter])
    o_out[...] = (probs[...] * ffn).astype(BF16)
    o_grad[...] = dot(place[...], back[:, quarter:]).astype(BF16)
    part_col = jnp.sum(ffn * cot[:, columns].astype(F32), axis=1, keepdims=True)
    part_row = jnp.sum(jnp.where(diag, part_col, 0.0), axis=0, keepdims=True)
    parts[n] = jnp.broadcast_to(part_row, parts.shape[1:])
    sent = []
    for k, peer in enumerate((core_peer, row_peer, far_peer)):
        copy = remote(parts.at[n], parts.at[n], p_send.at[k], p_recv.at[n], me, peer)
        copy.start()
        sent.append(copy)
    finish(nf - 1)
    for peer in (core_peer, row_peer, far_peer):
        await_bytes(parts.at[peer], p_recv.at[peer])
    o_prob[...] = (parts[0] + parts[1] + parts[2] + parts[3])[:1]

    for copy in (*sent, to_row, to_core, relay, t1_near, t1_far, t2):
        copy.wait_send()
    await_bytes(sendbuf.at[pl.ds(0, slots - CAP)], a_send)
    await_bytes(fo.at[pl.ds(0, rows - CAP)], b_send)

    @pl.loop(0, nf)
    def _(f):
        for q in range(4):
            @pl.when(m != q)
            def _():
                await_bytes(stage.at[f, q], rs_send.at[f, q])

            @pl.when((m < 3) & (m >= q))
            def _():
                await_bytes(wall.at[f, q], ag_send.at[0, f, q])

            @pl.when((m > 0) & (m <= q))
            def _():
                await_bytes(wall.at[f, q], ag_send.at[1, f, q])


def shards(wide, tokens, cotangent, expert_ids, route_prob, gate_weight, up_weight, down_weight):
    toks, width = tokens.shape
    quarter, ff = gate_weight.shape
    experts = wide // 4
    slots = experts * CAP
    rows = wide // 4 * CAP
    chunk = min(CHUNK, quarter)
    nf = -(-ff // chunk)
    vmem, dma = pltpu.VMEM, pltpu.SemaphoreType.DMA
    spec = pl.BlockSpec(memory_space=pltpu.VMEM)
    grad = jax.ShapeDtypeStruct((quarter, ff), F32)
    two = 2 * quarter
    outs = pl.pallas_call(
        kernel,
        out_shape=(
            jax.ShapeDtypeStruct((toks, quarter), BF16),
            jax.ShapeDtypeStruct((toks, quarter), BF16),
            jax.ShapeDtypeStruct((1, toks), F32),
            grad, grad, grad,
        ),
        in_specs=[spec] * 7,
        out_specs=(spec,) * 6,
        scratch_shapes=[
            vmem((nf, 4, 3, quarter, chunk), BF16),
            vmem((slots, two), BF16),
            vmem((4, rows, two), BF16),
            vmem((4, two, rows), BF16),
            vmem((3, rows, chunk), F32),
            vmem((3, rows, chunk), BF16),
            vmem((4, rows, quarter), F32),
            vmem((4, rows, quarter), F32),
            vmem((nf, 4, 3, quarter, chunk), F32),
            vmem((nf, 4, 3, quarter, chunk), BF16),
            vmem((nf, 4, 3, quarter, chunk), BF16),
            vmem((nf, 4, 3, quarter, chunk), BF16),
            vmem((2, rows, two), BF16),
            vmem((2, rows, two), BF16),
            vmem((rows, two), BF16),
            vmem((rows, two), BF16),
            vmem((rows, two), BF16),
            vmem((slots, two), BF16),
            vmem((toks, slots), BF16),
            vmem((toks, quarter), F32),
            vmem((4, 8, toks), F32),
            dma((2, nf, 4)), dma((nf, 4)), dma((nf, 4)), dma((2, nf, 4)),
            dma, dma, dma((2,)), dma((3,)), dma((4,)),
            dma((2,)), dma((2,)), dma, dma, dma, dma, dma((3,)), dma((4,)),
        ],
        compiler_params=pltpu.CompilerParams(
            collective_id=0, has_side_effects=True, vmem_limit_bytes=63000 * 1024
        ),
    )(
        tokens, cotangent, expert_ids, route_prob.reshape(1, toks),
        gate_weight, up_weight, down_weight,
    )
    return outs[0], outs[1], outs[2].reshape(toks), outs[3], outs[4], outs[5]


def solution(mesh):
    in_specs = (
        P("wide", None),
        P("wide", None),
        P("wide", None),
        P("wide"),
        P("wide", "narrow"),
        P("wide", "narrow"),
        P("wide", "narrow"),
    )
    out_specs = (
        P("wide", "narrow"),
        P("wide", "narrow"),
        P("wide"),
        P("wide", "narrow"),
        P("wide", "narrow"),
        P("wide", "narrow"),
    )
    return jax.shard_map(
        functools.partial(shards, mesh.shape["wide"]),
        mesh=mesh, in_specs=in_specs, out_specs=out_specs, check_vma=False,
    )
```

```python
import functools

import jax
import jax.numpy as jnp
from jax import lax
from jax.experimental import pallas as pl
from jax.experimental.pallas import tpu as pltpu
from jax.sharding import PartitionSpec as P

CAP = 16
F32 = jnp.float32
BF16 = jnp.bfloat16


def dot(a, b):
    return lax.dot_general(a, b, (((1,), (0,)), ((), ())), preferred_element_type=F32)


def dot_t(a, b):
    return lax.dot_general(a, b, (((1,), (1,)), ((), ())), preferred_element_type=F32)


def cuts(ff):
    step = ff // 4 if ff % 64 == 0 else ff
    return [(low, step) for low in range(0, ff, step)]


def piece_count(blocks):
    return min(4, blocks)


def kernel(
    tok, cot, ids, prob, wg, wu, wd,
    o_out, o_grad, o_prob, o_gg, o_gu, o_gd,
    wall, sendbuf, x4, act_t, pre, act3, out_acc, in_acc, gloc, r_right, r_left, stage,
    t1s, t1r, t2s, t2r, fo, back, place, probs, parts,
    ag_send, ag_recv, rs_send, rs_recv, a_send, a_recv, l_sem, n_send, n_recv,
    t1_send, t1_recv, t2_send, t2_recv, b_send, b_recv, p_send, p_recv, o_sem, enter,
):
    toks, width = tok.shape
    _, _, ff, quarter = wall.shape
    chunks = cuts(ff)
    nf = len(chunks)
    experts = sendbuf.shape[0] // CAP
    rows = x4.shape[1]
    blocks = rows // CAP
    pieces = piece_count(blocks)
    piece_blocks = blocks // pieces
    piece_rows = rows // pieces
    turns = (0, 1, 3, 2)[:pieces] if pieces > 2 else tuple(range(pieces))
    x_size = min(4, experts // 2)
    y_size = experts // 2 // x_size
    me = lax.axis_index("wide")
    n = lax.axis_index("narrow")
    m = lax.rem(me, 4)
    e0 = lax.div(me, 4)
    half = lax.rem(e0, 2)
    group = lax.div(me, 8)
    i0 = group * 2
    own_piece = lax.div(i0, piece_blocks)
    x_at, y_at, z_at = lax.rem(group, x_size), lax.div(group, x_size), lax.rem(me, 8)
    core_peer = n + 1 - 2 * lax.rem(n, 2)
    row_peer = lax.rem(n + 2, 4)
    far_peer = 3 - n

    def dest_of(e):
        h = lax.rem(e + half, 2)
        return 4 * e + m + h * (3 - 2 * m), i0 + h

    def source_of(i):
        h = lax.rem(i, 2)
        return lax.div(i, 2) * 8 + lax.rem(half + h, 2) * 4 + m + h * (3 - 2 * m)

    def remote(src, dst, ssem, rsem, wide, narrow):
        return pltpu.make_async_remote_copy(
            src_ref=src, dst_ref=dst, send_sem=ssem, recv_sem=rsem,
            device_id={"wide": wide, "narrow": narrow}, device_id_type=pl.DeviceIdType.MESH,
        )

    def await_bytes(ref, sem):
        pltpu.make_async_copy(ref, ref, sem).wait()

    owned = [
        pltpu.make_async_copy(ref, wall.at[m, k], l_sem.at[2 + k])
        for k, ref in enumerate((wg, wu, wd))
    ]
    for copy in owned:
        copy.start()

    barrier = pltpu.get_barrier_semaphore()

    def signal(wide, narrow):
        pl.semaphore_signal(
            barrier, inc=1, device_id={"wide": wide, "narrow": narrow},
            device_id_type=pl.DeviceIdType.MESH,
        )

    for turn in range(1, 8):
        signal(8 * group + lax.rem(z_at + turn, 8), n)
    for peer in (core_peer, row_peer, far_peer):
        signal(me, peer)
    along_x = [
        (y_at * x_size + lax.rem(x_at + turn, x_size)) * 8 + z_at for turn in range(1, x_size)
    ]
    along_y = [
        (lax.rem(y_at + turn, y_size) * x_size + x_at) * 8 + z_at for turn in range(1, y_size)
    ]
    for peer in (*along_x, *along_y):
        signal(peer, n)

    def piece(ref, f, q):
        low, size = chunks[f]
        return ref.at[q, :, pl.ds(low, size)]

    def ag_right(f, q):
        return remote(
            piece(wall, f, q), piece(wall, f, q), ag_send.at[0, f, q], ag_recv.at[f, q], me + 1, n
        )

    def ag_left(f, q):
        return remote(
            piece(wall, f, q), piece(wall, f, q), ag_send.at[1, f, q], ag_recv.at[f, q], me - 1, n
        )

    def ag_own(f):
        @pl.when(m < 3)
        def _():
            ag_right(f, m).start()

        @pl.when(m > 0)
        def _():
            ag_left(f, m).start()

    def ag_await(f, q):
        await_bytes(piece(wall, f, q), ag_recv.at[f, q])

    def ag_late(fs):
        for f in fs:
            @pl.when(m == 0)
            def _():
                ag_right(f, 0).start()

            @pl.when(m == 3)
            def _():
                ag_left(f, 3).start()

    def mid_fill(f):
        for own, near, send, back_near, back_far, send_back in (
            (1, 0, ag_right, 2, 3, ag_left),
            (2, 3, ag_left, 1, 0, ag_right),
        ):
            @pl.when(m == own)
            def _():
                ag_await(f, near)
                send(f, near).start()
                if f + 2 < nf:
                    send(f + 2, own).start()
                ag_await(f, back_near)
                send_back(f, back_near).start()
                ag_await(f, back_far)
                send_back(f, back_far).start()
                if f + 2 < nf:
                    send_back(f + 2, own).start()

    def end_fill(f):
        for own, others in ((0, (1, 2, 3)), (3, (2, 1, 0))):
            @pl.when(m == own)
            def _():
                for q in others:
                    ag_await(f, q)

    def pass_on(sem, peers):
        for peer in peers:
            pl.semaphore_signal(
                sem, inc=1, device_id={"wide": peer, "narrow": n},
                device_id_type=pl.DeviceIdType.MESH,
            )

    for copy in owned:
        copy.wait()
    pl.semaphore_wait(barrier, 10 + len(along_x) + len(along_y))
    pass_on(enter.at[0], along_x)
    ag_own(0)
    ag_own(1)

    def iota(shape, axis):
        return lax.broadcasted_iota(jnp.int32, shape, axis).astype(F32)

    slots = experts * CAP
    row_i, col_i = iota((toks, toks), 0), iota((toks, toks), 1)
    diag = row_i == col_i
    idf = ids[...].astype(F32)
    onehot = jnp.where(iota((experts, toks), 0) == idf, 1.0, 0.0)
    before = jnp.where(row_i < col_i, 1.0, 0.0).astype(BF16)
    rank = jnp.sum(dot(onehot.astype(BF16), before) * onehot, axis=0, keepdims=True)
    slot_row = idf * CAP + rank
    slot = jnp.sum(jnp.where(diag, slot_row, 0.0), axis=1, keepdims=True)
    place[...] = jnp.where(iota((toks, slots), 1) == slot, 1.0, 0.0).astype(BF16)
    prob_col = jnp.sum(jnp.where(diag, prob[...], 0.0), axis=1, keepdims=True)
    probs[...] = jnp.broadcast_to(prob_col, (toks, quarter))
    columns = pl.ds(pl.multiple_of(n * quarter, quarter), quarter)
    pick = jnp.where(iota((slots, toks), 0) == slot_row, 1.0, 0.0).astype(BF16)
    scaled = (prob_col * cot[:, columns].astype(F32)).astype(BF16)
    sendbuf[:, :quarter] = dot(pick, tok[:, columns]).astype(BF16)
    sendbuf[:, quarter:] = dot(pick, scaled).astype(BF16)

    if along_x:
        pl.semaphore_wait(enter.at[0], len(along_x))
    if along_y:
        pass_on(enter.at[1], along_y)
        pl.semaphore_wait(enter.at[1], len(along_y))

    def rows_at(i):
        return pl.ds(pl.multiple_of(i * CAP, CAP), CAP)

    def rows_of(p):
        return pl.ds(pl.multiple_of(p * piece_rows, piece_rows), piece_rows)

    def piece_at(turn):
        return lax.rem(own_piece + turn, pieces)

    pltpu.make_async_copy(
        sendbuf.at[rows_at(e0)], x4.at[n, rows_at(i0)], a_recv.at[own_piece]
    ).start()

    @pl.loop(1, experts)
    def _(j):
        e = lax.rem(e0 + j, experts)
        wide, block = dest_of(e)
        remote(
            sendbuf.at[rows_at(e)], x4.at[n, rows_at(block)], a_send, a_recv.at[own_piece], wide, n
        ).start()

    def x_copy(k, slot, turn, peer):
        part = x4.at[slot, rows_of(piece_at(turn))]
        return remote(
            part, part, n_send.at[k, piece_at(turn)], n_recv.at[slot, piece_at(turn)], me, peer
        )

    def x_await(slot, turn):
        p = piece_at(turn)
        await_bytes(x4.at[slot, rows_of(p)], n_recv.at[slot, p])

    x_sent = []

    def x_share(turn):
        await_bytes(x4.at[n, rows_of(piece_at(turn))], a_recv.at[piece_at(turn)])
        for k, peer in ((1, row_peer), (0, core_peer)):
            copy = x_copy(k, n, turn, peer)
            copy.start()
            x_sent.append(copy)

    def x_relay(turn):
        x_await(row_peer, turn)
        copy = x_copy(2, row_peer, turn, core_peer)
        copy.start()
        x_sent.append(copy)

    out_acc[...] = jnp.zeros_like(out_acc)
    in_acc[...] = jnp.zeros_like(in_acc)
    ag_late(range(2, nf))
    mid_fill(0)
    for turn in turns:
        x_share(turn)
    mid_fill(1)
    for turn in turns:
        x_relay(turn)
    for slot in (core_peer, far_peer):
        for turn in turns:
            x_await(slot, turn)

    def rs_right(f, q):
        return remote(
            piece(stage, f, q), piece(r_right, f, q), rs_send.at[f, q], rs_recv.at[0, f, q], me + 1, n
        )

    def rs_left(f, q):
        return remote(
            piece(stage, f, q), piece(r_left, f, q), rs_send.at[f, q], rs_recv.at[1, f, q], me - 1, n
        )

    def rs_first(f):
        low, size = chunks[f]
        part = pl.ds(low, size)

        @pl.when(m == 0)
        def _():
            for q in (3, 2, 1):
                stage[q, :, part] = gloc[q, :, part].astype(BF16)
                rs_right(f, q).start()

        @pl.when(m == 3)
        def _():
            for q in (0, 1, 2):
                stage[q, :, part] = gloc[q, :, part].astype(BF16)
                rs_left(f, q).start()

    def relay(f, source, k, q, send):
        low, size = chunks[f]
        part = pl.ds(low, size)
        await_bytes(piece(source, f, q), rs_recv.at[k, f, q])
        stage[q, :, part] = (gloc[q, :, part] + source[q, :, part].astype(F32)).astype(BF16)
        send(f, q).start()

    def relay_a(f, k):
        @pl.when(m == 1)
        def _():
            relay(f, r_right, 0, 3 - k, rs_right)

        @pl.when(m == 2)
        def _():
            relay(f, r_left, 1, k, rs_left)

    def relay_b(f):
        @pl.when(m == 1)
        def _():
            relay(f, r_left, 1, 0, rs_left)

        @pl.when(m == 2)
        def _():
            relay(f, r_right, 0, 3, rs_right)

    step_rows = min(64, rows)
    eye = jnp.where(iota((256, 256), 0) == iota((256, 256), 1), 1.0, 0.0).astype(BF16)

    for f, (low, size) in enumerate(chunks):
        end_fill(f)
        units = pl.ds(low, size)
        for k, first in ((0, 0), (1, 0), (2, quarter)):
            total = dot_t(x4[0, :, first : first + quarter], wall[0, k, units])
            for q in range(1, 4):
                total += dot_t(x4[q, :, first : first + quarter], wall[q, k, units])
            pre[k, :, :size] = total

        @pl.loop(0, rows // step_rows)
        def _(r):
            part = pl.ds(pl.multiple_of(r * step_rows, step_rows), step_rows)
            gate, up, d_hidden = pre[0, part, :size], pre[1, part, :size], pre[2, part, :size]
            sigma = jax.nn.sigmoid(gate)
            active = gate * sigma
            d_gate = d_hidden * up * sigma * (1.0 + gate * (1.0 - sigma))
            act3[0, part, :size] = (active * up).astype(BF16)
            act3[1, part, :size] = d_gate.astype(BF16)
            act3[2, part, :size] = (d_hidden * active).astype(BF16)

        for k in range(3):
            act_t[k, :size] = dot_t(eye[:size, :size], act3[k, :, :size]).astype(BF16)

        @pl.loop(0, 4)
        def _(q):
            gloc[q, 0, units] = dot(act_t[1, :size], x4[q, :, :quarter])
            gloc[q, 1, units] = dot(act_t[2, :size], x4[q, :, :quarter])
            gloc[q, 2, units] = dot(act_t[0, :size], x4[q, :, quarter:])

        rs_first(f)

        @pl.loop(0, 4)
        def _(q):
            out_acc[q] += dot(act3[0, :, :size], wall[q, 2, units])
            in_acc[q] += dot(act3[1, :, :size], wall[q, 0, units]) + dot(
                act3[2, :, :size], wall[q, 1, units]
            )

        if f + 2 < nf:
            mid_fill(f + 2)
        if f == nf - 2:
            for k in range(2):
                relay_a(0, k)

    def both(q, part):
        return jnp.concatenate([out_acc[q, part], in_acc[q, part]], axis=1)

    back_turns = (2, 1, 3, 0) if pieces == 4 else turns
    t1, t2 = {}, {}
    for k, q in ((1, far_peer), (0, core_peer)):
        for turn in back_turns:
            p = piece_at(turn)
            part = rows_of(p)
            t1s[k, part] = both(q, part).astype(BF16)
            t1[k, turn] = remote(
                t1s.at[k, part], t1r.at[k, part], t1_send.at[k, p], t1_recv.at[k, p], me, core_peer
            )
            t1[k, turn].start()
    for k in range(2):
        relay_a(1, k)
    for turn in back_turns:
        p = piece_at(turn)
        part = rows_of(p)
        t1[1, turn].wait_recv()
        t2s[part] = (both(row_peer, part) + t1r[1, part].astype(F32)).astype(BF16)
        t2[turn] = remote(t2s.at[part], t2r.at[part], t2_send.at[p], t2_recv.at[p], me, row_peer)
        t2[turn].start()

    def send_back(turn):
        p = piece_at(turn)
        part = rows_of(p)
        t1[0, turn].wait_recv()
        t2[turn].wait_recv()
        total = both(n, part) + t1r[0, part].astype(F32) + t2r[part].astype(F32)
        fo[part] = total.astype(BF16)

        @pl.loop(0, piece_blocks)
        def _(j):
            i = p * piece_blocks + j

            @pl.when(i == i0)
            def _():
                pltpu.make_async_copy(fo.at[rows_at(i)], back.at[rows_at(e0)], b_recv).start()

            @pl.when(i != i0)
            def _():
                remote(
                    fo.at[rows_at(i)], back.at[rows_at(e0)], b_send, b_recv, source_of(i), n
                ).start()

    half_turns = len(back_turns) // 2
    relay_b(0)
    for turn in back_turns[:half_turns]:
        send_back(turn)
    relay_b(1)
    for turn in back_turns[half_turns:]:
        send_back(turn)
    for f in range(2, nf):
        for k in range(2):
            relay_a(f, k)
        if f < nf - 1:
            relay_b(f)
    relay_b(nf - 1)

    written = []

    def finish(f):
        low, size = chunks[f]
        part = pl.ds(low, size)

        @pl.when(m > 0)
        def _():
            await_bytes(piece(r_right, f, m), rs_recv.at[0, f, m])
            gloc[m, :, part] += r_right[m, :, part].astype(F32)

        @pl.when(m < 3)
        def _():
            await_bytes(piece(r_left, f, m), rs_recv.at[1, f, m])
            gloc[m, :, part] += r_left[m, :, part].astype(F32)

        for k, ref in enumerate((o_gg, o_gu, o_gd)):
            copy = pltpu.make_async_copy(gloc.at[m, k, part], ref.at[part], o_sem.at[k, f])
            copy.start()
            written.append(copy)

    for f in range(nf - 1):
        finish(f)

    await_bytes(back, b_recv)
    ffn = dot(place[...], back[:, :quarter])
    o_out[...] = (probs[...] * ffn).astype(BF16)
    o_grad[...] = dot(place[...], back[:, quarter:]).astype(BF16)
    part_col = jnp.sum(ffn * cot[:, columns].astype(F32), axis=1, keepdims=True)
    part_row = jnp.sum(jnp.where(diag, part_col, 0.0), axis=0, keepdims=True)
    parts[n] = jnp.broadcast_to(part_row, parts.shape[1:])
    sent = []
    for k, peer in enumerate((core_peer, row_peer, far_peer)):
        copy = remote(parts.at[n], parts.at[n], p_send.at[k], p_recv.at[n], me, peer)
        copy.start()
        sent.append(copy)
    finish(nf - 1)
    for peer in (core_peer, row_peer, far_peer):
        await_bytes(parts.at[peer], p_recv.at[peer])
    o_prob[...] = (parts[0] + parts[1] + parts[2] + parts[3])[:1]

    for copy in (*sent, *x_sent, *t1.values(), *t2.values()):
        copy.wait_send()
    for copy in written:
        copy.wait()
    await_bytes(sendbuf.at[pl.ds(0, slots - CAP)], a_send)
    await_bytes(fo.at[pl.ds(0, rows - CAP)], b_send)

    for f in range(nf):
        for q in range(4):
            @pl.when(m != q)
            def _():
                await_bytes(piece(stage, f, q), rs_send.at[f, q])

            @pl.when((m < 3) & (m >= q))
            def _():
                await_bytes(piece(wall, f, q), ag_send.at[0, f, q])

            @pl.when((m > 0) & (m <= q))
            def _():
                await_bytes(piece(wall, f, q), ag_send.at[1, f, q])


def shards(wide, tokens, cotangent, expert_ids, route_prob, gate_weight, up_weight, down_weight):
    toks, width = tokens.shape
    quarter, ff = gate_weight.shape
    experts = wide // 4
    slots = experts * CAP
    rows = wide // 4 * CAP
    nf = len(cuts(ff))
    chunk = cuts(ff)[0][1]
    pieces = piece_count(experts)
    any_spec = pl.BlockSpec(memory_space=pl.ANY)
    vmem, dma = pltpu.VMEM, pltpu.SemaphoreType.DMA
    spec = pl.BlockSpec(memory_space=pltpu.VMEM)
    grad = jax.ShapeDtypeStruct((ff, quarter), F32)
    two = 2 * quarter
    outs = pl.pallas_call(
        kernel,
        out_shape=(
            jax.ShapeDtypeStruct((toks, quarter), BF16),
            jax.ShapeDtypeStruct((toks, quarter), BF16),
            jax.ShapeDtypeStruct((1, toks), F32),
            grad, grad, grad,
        ),
        in_specs=[spec] * 4 + [any_spec] * 3,
        out_specs=(spec,) * 3 + (any_spec,) * 3,
        scratch_shapes=[
            vmem((4, 3, ff, quarter), BF16),
            vmem((slots, two), BF16),
            vmem((4, rows, two), BF16),
            vmem((3, chunk, rows), BF16),
            vmem((3, rows, chunk), F32),
            vmem((3, rows, chunk), BF16),
            vmem((4, rows, quarter), F32),
            vmem((4, rows, quarter), F32),
            vmem((4, 3, ff, quarter), F32),
            vmem((4, 3, ff, quarter), BF16),
            vmem((4, 3, ff, quarter), BF16),
            vmem((4, 3, ff, quarter), BF16),
            vmem((2, rows, two), BF16),
            vmem((2, rows, two), BF16),
            vmem((rows, two), BF16),
            vmem((rows, two), BF16),
            vmem((rows, two), BF16),
            vmem((slots, two), BF16),
            vmem((toks, slots), BF16),
            vmem((toks, quarter), F32),
            vmem((4, 8, toks), F32),
            dma((2, nf, 4)), dma((nf, 4)), dma((nf, 4)), dma((2, nf, 4)),
            dma, dma((pieces,)), dma((5,)), dma((3, pieces)), dma((4, pieces)),
            dma((2, pieces)), dma((2, pieces)), dma((pieces,)), dma((pieces,)),
            dma, dma, dma((3,)), dma((4,)), dma((3, nf)), pltpu.SemaphoreType.REGULAR((2,)),
        ],
        compiler_params=pltpu.CompilerParams(
            collective_id=0, has_side_effects=True, vmem_limit_bytes=63000 * 1024
        ),
    )(
        tokens, cotangent, expert_ids.reshape(1, toks), route_prob.reshape(1, toks),
        gate_weight.T, up_weight.T, down_weight.T,
    )
    return outs[0], outs[1], outs[2].reshape(toks), outs[3].T, outs[4].T, outs[5].T


def solution(mesh):
    in_specs = (
        P("wide", None),
        P("wide", None),
        P("wide", None),
        P("wide"),
        P("wide", "narrow"),
        P("wide", "narrow"),
        P("wide", "narrow"),
    )
    out_specs = (
        P("wide", "narrow"),
        P("wide", "narrow"),
        P("wide"),
        P("wide", "narrow"),
        P("wide", "narrow"),
        P("wide", "narrow"),
    )
    return jax.shard_map(
        functools.partial(shards, mesh.shape["wide"]),
        mesh=mesh, in_specs=in_specs, out_specs=out_specs, check_vma=False,
    )
```

```python
import functools

import jax
import jax.numpy as jnp
from jax import lax
from jax.experimental import pallas as pl
from jax.experimental.pallas import tpu as pltpu
from jax.sharding import PartitionSpec as P

CAP = 16
F32 = jnp.float32
BF16 = jnp.bfloat16


def dot(a, b):
    return lax.dot_general(a, b, (((1,), (0,)), ((), ())), preferred_element_type=F32)


def dot_t(a, b):
    return lax.dot_general(a, b, (((1,), (1,)), ((), ())), preferred_element_type=F32)


def cuts(ff):
    step = ff // 4
    return [(low, step) for low in range(0, ff, step)]


def piece_count(blocks):
    return min(4, blocks)


def kernel(
    tok, cot, ids, prob, wg, wu, wd,
    o_rows, o_prob, o_weights,
    wall, sendbuf, x4, act_t, pre, act3, out_acc, in_acc, gloc, r_right, r_left, stage,
    t1s, t1r, t2s, t2r, fo, back, place, probs, parts, rows_out, prob_out,
    ag_send, ag_recv, rs_send, rs_recv, a_send, a_recv, l_sem, n_send, n_recv,
    t1_send, t1_recv, t2_send, t2_recv, b_send, b_recv, p_send, p_recv, o_sem, enter,
):
    toks, width = tok.shape
    _, _, ff, quarter = wall.shape
    chunks = cuts(ff)
    nf = len(chunks)
    experts = sendbuf.shape[0] // CAP
    rows = x4.shape[1]
    blocks = rows // CAP
    pieces = piece_count(blocks)
    piece_blocks = blocks // pieces
    piece_rows = rows // pieces
    turns = (0, 1, 3, 2)[:pieces] if pieces > 2 else tuple(range(pieces))
    x_size = min(4, experts // 2)
    y_size = experts // 2 // x_size
    me = lax.axis_index("wide")
    n = lax.axis_index("narrow")
    m = lax.rem(me, 4)
    e0 = lax.div(me, 4)
    half = lax.rem(e0, 2)
    group = lax.div(me, 8)
    i0 = group * 2
    own_piece = lax.div(i0, piece_blocks)
    x_at, y_at, z_at = lax.rem(group, x_size), lax.div(group, x_size), lax.rem(me, 8)
    core_peer = n + 1 - 2 * lax.rem(n, 2)
    row_peer = lax.rem(n + 2, 4)
    far_peer = 3 - n

    def dest_of(e):
        h = lax.rem(e + half, 2)
        return 4 * e + m + h * (3 - 2 * m), i0 + h

    def source_of(i):
        h = lax.rem(i, 2)
        return lax.div(i, 2) * 8 + lax.rem(half + h, 2) * 4 + m + h * (3 - 2 * m)

    def remote(src, dst, ssem, rsem, wide, narrow):
        return pltpu.make_async_remote_copy(
            src_ref=src, dst_ref=dst, send_sem=ssem, recv_sem=rsem,
            device_id={"wide": wide, "narrow": narrow}, device_id_type=pl.DeviceIdType.MESH,
        )

    def await_bytes(ref, sem):
        pltpu.make_async_copy(ref, ref, sem).wait()

    owned = [
        pltpu.make_async_copy(ref, wall.at[m, k], l_sem.at[2 + k])
        for k, ref in enumerate((wg, wu, wd))
    ]
    for copy in owned:
        copy.start()

    barrier = pltpu.get_barrier_semaphore()

    def signal(wide, narrow):
        pl.semaphore_signal(
            barrier, inc=1, device_id={"wide": wide, "narrow": narrow},
            device_id_type=pl.DeviceIdType.MESH,
        )

    for turn in range(1, 8):
        signal(8 * group + lax.rem(z_at + turn, 8), n)
    for peer in (core_peer, row_peer, far_peer):
        signal(me, peer)
    along_x = [
        (y_at * x_size + lax.rem(x_at + turn, x_size)) * 8 + z_at for turn in range(1, x_size)
    ]
    along_y = [
        (lax.rem(y_at + turn, y_size) * x_size + x_at) * 8 + z_at for turn in range(1, y_size)
    ]
    for peer in (*along_x, *along_y):
        signal(peer, n)

    def piece(ref, f, q):
        low, size = chunks[f]
        return ref.at[q, :, pl.ds(low, size)]

    def ag_right(f, q):
        return remote(
            piece(wall, f, q), piece(wall, f, q), ag_send.at[0, f, q], ag_recv.at[f, q], me + 1, n
        )

    def ag_left(f, q):
        return remote(
            piece(wall, f, q), piece(wall, f, q), ag_send.at[1, f, q], ag_recv.at[f, q], me - 1, n
        )

    def ag_own(f):
        @pl.when(m < 3)
        def _():
            ag_right(f, m).start()

        @pl.when(m > 0)
        def _():
            ag_left(f, m).start()

    def ag_await(f, q):
        await_bytes(piece(wall, f, q), ag_recv.at[f, q])

    def ag_late(fs):
        for f in fs:
            @pl.when(m == 0)
            def _():
                ag_right(f, 0).start()

            @pl.when(m == 3)
            def _():
                ag_left(f, 3).start()

    middle = (
        (1, 0, ag_right, 2, 3, ag_left),
        (2, 3, ag_left, 1, 0, ag_right),
    )

    def near_fill(f):
        for own, near, send, _, _, _ in middle:
            @pl.when(m == own)
            def _():
                ag_await(f, near)
                send(f, near).start()
                if f + 2 < nf:
                    send(f + 2, own).start()

    def back_fill(f):
        for own, _, _, near, far, send in middle:
            @pl.when(m == own)
            def _():
                for q in (near, far):
                    ag_await(f, q)
                    send(f, q).start()
                if f + 2 < nf:
                    send(f + 2, own).start()

    def end_fill(f):
        for own, others in ((0, (1, 2, 3)), (3, (2, 1, 0))):
            @pl.when(m == own)
            def _():
                for q in others:
                    ag_await(f, q)

    def pass_on(sem, peers):
        for peer in peers:
            pl.semaphore_signal(
                sem, inc=1, device_id={"wide": peer, "narrow": n},
                device_id_type=pl.DeviceIdType.MESH,
            )

    pl.semaphore_wait(barrier, 10 + len(along_x) + len(along_y))
    pass_on(enter.at[0], along_x)
    for copy in owned:
        copy.wait()
    ag_own(0)
    ag_own(1)
    if along_x:
        pl.semaphore_wait(enter.at[0], len(along_x))
    pass_on(enter.at[1], along_y)

    def iota(shape, axis):
        return lax.broadcasted_iota(jnp.int32, shape, axis).astype(F32)

    slots = experts * CAP
    row_i, col_i = iota((toks, toks), 0), iota((toks, toks), 1)
    diag = row_i == col_i
    idf = ids[...].astype(F32)
    onehot = jnp.where(iota((experts, toks), 0) == idf, 1.0, 0.0)
    before = jnp.where(row_i < col_i, 1.0, 0.0).astype(BF16)
    rank = jnp.sum(dot(onehot.astype(BF16), before) * onehot, axis=0, keepdims=True)
    slot_row = idf * CAP + rank
    slot = jnp.sum(jnp.where(diag, slot_row, 0.0), axis=1, keepdims=True)
    place[...] = jnp.where(iota((toks, slots), 1) == slot, 1.0, 0.0).astype(BF16)
    prob_col = jnp.sum(jnp.where(diag, prob[...], 0.0), axis=1, keepdims=True)
    probs[...] = jnp.broadcast_to(prob_col, (toks, quarter))
    columns = pl.ds(pl.multiple_of(n * quarter, quarter), quarter)
    pick = jnp.where(iota((slots, toks), 0) == slot_row, 1.0, 0.0).astype(BF16)
    scaled = (prob_col * cot[:, columns].astype(F32)).astype(BF16)
    sendbuf[:, :quarter] = dot(pick, tok[:, columns]).astype(BF16)
    sendbuf[:, quarter:] = dot(pick, scaled).astype(BF16)

    if along_y:
        pl.semaphore_wait(enter.at[1], len(along_y))

    def rows_at(i):
        return pl.ds(pl.multiple_of(i * CAP, CAP), CAP)

    def rows_of(p):
        return pl.ds(pl.multiple_of(p * piece_rows, piece_rows), piece_rows)

    def piece_at(turn):
        return lax.rem(own_piece + turn, pieces)

    pltpu.make_async_copy(
        sendbuf.at[rows_at(e0)], x4.at[n, rows_at(i0)], a_recv.at[own_piece]
    ).start()

    def send_block(j):
        e = lax.rem(e0 + j, experts)
        wide, block = dest_of(e)
        remote(
            sendbuf.at[rows_at(e)], x4.at[n, rows_at(block)], a_send, a_recv.at[own_piece], wide, n
        ).start()

    pl.loop(experts // 2, experts)(send_block)
    pl.loop(1, experts // 2)(send_block)

    def x_copy(k, slot, turn, peer):
        part = x4.at[slot, rows_of(piece_at(turn))]
        return remote(
            part, part, n_send.at[k, piece_at(turn)], n_recv.at[slot, piece_at(turn)], me, peer
        )

    def x_await(slot, turn):
        p = piece_at(turn)
        await_bytes(x4.at[slot, rows_of(p)], n_recv.at[slot, p])

    x_sent = []

    def x_share(turn):
        await_bytes(x4.at[n, rows_of(piece_at(turn))], a_recv.at[piece_at(turn)])
        for k, peer in ((1, row_peer), (0, core_peer)):
            copy = x_copy(k, n, turn, peer)
            copy.start()
            x_sent.append(copy)

    def x_relay(turn):
        x_await(row_peer, turn)
        copy = x_copy(2, row_peer, turn, core_peer)
        copy.start()
        x_sent.append(copy)

    out_acc[...] = jnp.zeros_like(out_acc)
    in_acc[...] = jnp.zeros_like(in_acc)
    near_fill(0)
    back_fill(0)
    for turn in turns:
        x_share(turn)
    ag_late(range(2, nf))
    near_fill(1)
    back_fill(1)
    for turn in turns:
        x_relay(turn)
    near_fill(2)
    near_fill(3)
    for slot in (core_peer, far_peer):
        for turn in turns:
            x_await(slot, turn)

    def rs_right(f, q):
        return remote(
            piece(stage, f, q), piece(r_right, f, q), rs_send.at[f, q], rs_recv.at[0, f, q], me + 1, n
        )

    def rs_left(f, q):
        return remote(
            piece(stage, f, q), piece(r_left, f, q), rs_send.at[f, q], rs_recv.at[1, f, q], me - 1, n
        )

    def rs_first(f, q):
        low, size = chunks[f]
        part = pl.ds(low, size)
        for own, send in ((0, rs_right), (3, rs_left)):
            @pl.when((m == own) & (q != own))
            def _():
                stage[q, :, part] = gloc[q, :, part].astype(BF16)
                send(f, q).start()

    def relay(f, source, k, q, send):
        low, size = chunks[f]
        part = pl.ds(low, size)
        await_bytes(piece(source, f, q), rs_recv.at[k, f, q])
        stage[q, :, part] = (gloc[q, :, part] + source[q, :, part].astype(F32)).astype(BF16)
        send(f, q).start()

    def relay_a(f, k):
        @pl.when(m == 1)
        def _():
            relay(f, r_right, 0, 3 - k, rs_right)

        @pl.when(m == 2)
        def _():
            relay(f, r_left, 1, k, rs_left)

    def relay_b(f):
        @pl.when(m == 1)
        def _():
            relay(f, r_left, 1, 0, rs_left)

        @pl.when(m == 2)
        def _():
            relay(f, r_right, 0, 3, rs_right)

    def both(q, part):
        return jnp.concatenate([out_acc[q, part], in_acc[q, part]], axis=1)

    back_turns = (2, 1, 3, 0) if pieces == 4 else turns
    t1, t2 = {}, {}

    def share_on_chip(k, q):
        for turn in back_turns:
            p = piece_at(turn)
            part = rows_of(p)
            t1s[k, part] = both(q, part).astype(BF16)
            t1[k, turn] = remote(
                t1s.at[k, part], t1r.at[k, part], t1_send.at[k, p], t1_recv.at[k, p], me, core_peer
            )
            t1[k, turn].start()

    step_rows = min(64, rows)
    eye = jnp.where(iota((256, 256), 0) == iota((256, 256), 1), 1.0, 0.0).astype(BF16)

    for f, (low, size) in enumerate(chunks):
        end_fill(f)
        units = pl.ds(low, size)
        for k, first in ((0, 0), (1, 0), (2, quarter)):
            total = dot_t(x4[0, :, first : first + quarter], wall[0, k, units])
            for q in range(1, 4):
                total += dot_t(x4[q, :, first : first + quarter], wall[q, k, units])
            pre[k, :, :size] = total

        @pl.loop(0, rows // step_rows)
        def _(r):
            part = pl.ds(pl.multiple_of(r * step_rows, step_rows), step_rows)
            gate, up, d_hidden = pre[0, part, :size], pre[1, part, :size], pre[2, part, :size]
            sigma = jax.nn.sigmoid(gate)
            active = gate * sigma
            d_gate = d_hidden * up * sigma * (1.0 + gate * (1.0 - sigma))
            act3[0, part, :size] = (active * up).astype(BF16)
            act3[1, part, :size] = d_gate.astype(BF16)
            act3[2, part, :size] = (d_hidden * active).astype(BF16)

        def transpose():
            for k in range(3):
                act_t[k, :size] = dot_t(eye[:size, :size], act3[k, :, :size]).astype(BF16)

        def gradients():
            @pl.loop(0, 4)
            def _(step):
                q = step + lax.div(3 - m, 2) * (3 - 2 * step)
                gloc[q, 0, units] = dot(act_t[1, :size], x4[q, :, :quarter])
                gloc[q, 1, units] = dot(act_t[2, :size], x4[q, :, :quarter])
                gloc[q, 2, units] = dot(act_t[0, :size], x4[q, :, quarter:])
                rs_first(f, q)

        def row_sum(q):
            out_acc[q] += dot(act3[0, :, :size], wall[q, 2, units])
            in_acc[q] += dot(act3[1, :, :size], wall[q, 0, units]) + dot(
                act3[2, :, :size], wall[q, 1, units]
            )

        if f < nf - 1:
            transpose()
            gradients()
            pl.loop(0, 4)(row_sum)
        else:
            for k, q in ((1, far_peer), (0, core_peer)):
                row_sum(q)
                share_on_chip(k, q)
            row_sum(row_peer)
            row_sum(n)
            transpose()
            gradients()
        if f < 2:
            relay_a(f, 0)
            back_fill(f + 2)
            relay_a(f, 1)
        if f == 2:
            relay_b(0)

    for turn in back_turns:
        p = piece_at(turn)
        part = rows_of(p)
        t1[1, turn].wait_recv()
        t2s[part] = (both(row_peer, part) + t1r[1, part].astype(F32)).astype(BF16)
        t2[turn] = remote(t2s.at[part], t2r.at[part], t2_send.at[p], t2_recv.at[p], me, row_peer)
        t2[turn].start()

    def send_back(turn):
        p = piece_at(turn)
        part = rows_of(p)
        t1[0, turn].wait_recv()
        t2[turn].wait_recv()
        total = both(n, part) + t1r[0, part].astype(F32) + t2r[part].astype(F32)
        fo[part] = total.astype(BF16)

        @pl.loop(0, piece_blocks)
        def _(j):
            i = p * piece_blocks + j

            @pl.when(i == i0)
            def _():
                pltpu.make_async_copy(fo.at[rows_at(i)], back.at[rows_at(e0)], b_recv).start()

            @pl.when(i != i0)
            def _():
                remote(
                    fo.at[rows_at(i)], back.at[rows_at(e0)], b_send, b_recv, source_of(i), n
                ).start()

    relay_a(2, 0)
    relay_b(1)
    relay_a(2, 1)
    for turn in back_turns:
        if turn == back_turns[-1]:
            relay_b(2)
            relay_a(3, 0)
        send_back(turn)
    relay_a(3, 1)
    relay_b(nf - 1)

    written = []

    def finish(f):
        low, size = chunks[f]
        part = pl.ds(low, size)

        @pl.when(m > 0)
        def _():
            await_bytes(piece(r_right, f, m), rs_recv.at[0, f, m])
            gloc[m, :, part] += r_right[m, :, part].astype(F32)

        @pl.when(m < 3)
        def _():
            await_bytes(piece(r_left, f, m), rs_recv.at[1, f, m])
            gloc[m, :, part] += r_left[m, :, part].astype(F32)

        copy = pltpu.make_async_copy(gloc.at[m, :, part], o_weights.at[:, part], o_sem.at[f])
        copy.start()
        written.append(copy)

    for f in range(nf - 1):
        finish(f)

    await_bytes(back, b_recv)
    ffn = dot(place[...], back[:, :quarter])
    rows_out[0] = (probs[...] * ffn).astype(BF16)
    rows_out[1] = dot(place[...], back[:, quarter:]).astype(BF16)
    copy = pltpu.make_async_copy(rows_out, o_rows, l_sem.at[0])
    copy.start()
    written.append(copy)
    part_col = jnp.sum(ffn * cot[:, columns].astype(F32), axis=1, keepdims=True)
    part_row = jnp.sum(jnp.where(diag, part_col, 0.0), axis=0, keepdims=True)
    parts[n] = jnp.broadcast_to(part_row, parts.shape[1:])
    sent = []
    for k, peer in enumerate((core_peer, row_peer, far_peer)):
        copy = remote(parts.at[n], parts.at[n], p_send.at[k], p_recv.at[n], me, peer)
        copy.start()
        sent.append(copy)
    for peer in (core_peer, row_peer, far_peer):
        await_bytes(parts.at[peer], p_recv.at[peer])
    prob_out[...] = (parts[0] + parts[1] + parts[2] + parts[3])[:1]
    copy = pltpu.make_async_copy(prob_out, o_prob, l_sem.at[1])
    copy.start()
    written.append(copy)
    finish(nf - 1)

    for copy in (*sent, *x_sent, *t1.values(), *t2.values()):
        copy.wait_send()
    for copy in written:
        copy.wait()
    await_bytes(sendbuf.at[pl.ds(0, slots - CAP)], a_send)
    await_bytes(fo.at[pl.ds(0, rows - CAP)], b_send)

    for f in range(nf):
        for q in range(4):
            @pl.when(m != q)
            def _():
                await_bytes(piece(stage, f, q), rs_send.at[f, q])

            @pl.when((m < 3) & (m >= q))
            def _():
                await_bytes(piece(wall, f, q), ag_send.at[0, f, q])

            @pl.when((m > 0) & (m <= q))
            def _():
                await_bytes(piece(wall, f, q), ag_send.at[1, f, q])


def shards(wide, tokens, cotangent, expert_ids, route_prob, gate_weight, up_weight, down_weight):
    toks, width = tokens.shape
    quarter, ff = gate_weight.shape
    experts = wide // 4
    slots = experts * CAP
    rows = wide // 4 * CAP
    nf = len(cuts(ff))
    chunk = cuts(ff)[0][1]
    pieces = piece_count(experts)
    any_spec = pl.BlockSpec(memory_space=pl.ANY)
    vmem, dma = pltpu.VMEM, pltpu.SemaphoreType.DMA
    spec = pl.BlockSpec(memory_space=pltpu.VMEM)
    two = 2 * quarter
    row_outs, prob_out, grads = pl.pallas_call(
        kernel,
        out_shape=(
            jax.ShapeDtypeStruct((2, toks, quarter), BF16),
            jax.ShapeDtypeStruct((1, toks), F32),
            jax.ShapeDtypeStruct((3, ff, quarter), F32),
        ),
        in_specs=[spec] * 4 + [any_spec] * 3,
        out_specs=(any_spec, any_spec, any_spec),
        scratch_shapes=[
            vmem((4, 3, ff, quarter), BF16),
            vmem((slots, two), BF16),
            vmem((4, rows, two), BF16),
            vmem((3, chunk, rows), BF16),
            vmem((3, rows, chunk), F32),
            vmem((3, rows, chunk), BF16),
            vmem((4, rows, quarter), F32),
            vmem((4, rows, quarter), F32),
            vmem((4, 3, ff, quarter), F32),
            vmem((4, 3, ff, quarter), BF16),
            vmem((4, 3, ff, quarter), BF16),
            vmem((4, 3, ff, quarter), BF16),
            vmem((2, rows, two), BF16),
            vmem((2, rows, two), BF16),
            vmem((rows, two), BF16),
            vmem((rows, two), BF16),
            vmem((rows, two), BF16),
            vmem((slots, two), BF16),
            vmem((toks, slots), BF16),
            vmem((toks, quarter), F32),
            vmem((4, 8, toks), F32),
            vmem((2, toks, quarter), BF16),
            vmem((1, toks), F32),
            dma((2, nf, 4)), dma((nf, 4)), dma((nf, 4)), dma((2, nf, 4)),
            dma, dma((pieces,)), dma((5,)), dma((3, pieces)), dma((4, pieces)),
            dma((2, pieces)), dma((2, pieces)), dma((pieces,)), dma((pieces,)),
            dma, dma, dma((3,)), dma((4,)), dma((nf,)), pltpu.SemaphoreType.REGULAR((2,)),
        ],
        compiler_params=pltpu.CompilerParams(
            collective_id=0, has_side_effects=True, vmem_limit_bytes=63000 * 1024
        ),
    )(
        tokens, cotangent, expert_ids.reshape(1, toks), route_prob.reshape(1, toks),
        gate_weight.T, up_weight.T, down_weight.T,
    )
    return row_outs[0], row_outs[1], prob_out.reshape(toks), grads[0].T, grads[1].T, grads[2].T


def solution(mesh):
    in_specs = (
        P("wide", None),
        P("wide", None),
        P("wide", None),
        P("wide"),
        P("wide", "narrow"),
        P("wide", "narrow"),
        P("wide", "narrow"),
    )
    out_specs = (
        P("wide", "narrow"),
        P("wide", "narrow"),
        P("wide"),
        P("wide", "narrow"),
        P("wide", "narrow"),
        P("wide", "narrow"),
    )
    return jax.shard_map(
        functools.partial(shards, mesh.shape["wide"]),
        mesh=mesh, in_specs=in_specs, out_specs=out_specs, check_vma=False,
    )
```

```python
import functools

import jax
import jax.numpy as jnp
from jax import lax
from jax.experimental import pallas as pl
from jax.experimental.pallas import tpu as pltpu
from jax.sharding import PartitionSpec as P

CAP = 16
F32 = jnp.float32
BF16 = jnp.bfloat16


def dot(a, b):
    return lax.dot_general(a, b, (((1,), (0,)), ((), ())), preferred_element_type=F32)


def dot_t(a, b):
    return lax.dot_general(a, b, (((1,), (1,)), ((), ())), preferred_element_type=F32)


def cuts(ff):
    step = ff // 4
    return [(low, step) for low in range(0, ff, step)]


def piece_count(blocks):
    return min(4, blocks)


def kernel(
    tok, cot, ids, prob, wg, wu, wd,
    o_rows, o_prob, o_weights,
    wall, sendbuf, x4, act_t, pre, act3, out_acc, in_acc, gloc, r_right, r_left, stage,
    t1s, t1r, t2s, t2r, fo, back, place, probs, parts, rows_out, prob_out,
    ag_send, ag_recv, rs_send, rs_recv, a_send, a_recv, l_sem, n_send, n_recv,
    t1_send, t1_recv, t2_send, t2_recv, b_send, b_recv, p_send, p_recv, o_sem, enter,
):
    toks, width = tok.shape
    _, _, ff, quarter = wall.shape
    chunks = cuts(ff)
    nf = len(chunks)
    experts = sendbuf.shape[0] // CAP
    rows = x4.shape[1]
    blocks = rows // CAP
    pieces = piece_count(blocks)
    piece_blocks = blocks // pieces
    piece_rows = rows // pieces
    turns = (0, 1, 3, 2)[:pieces] if pieces > 2 else tuple(range(pieces))
    x_size = min(4, experts // 2)
    y_size = experts // 2 // x_size
    me = lax.axis_index("wide")
    n = lax.axis_index("narrow")
    m = lax.rem(me, 4)
    e0 = lax.div(me, 4)
    half = lax.rem(e0, 2)
    group = lax.div(me, 8)
    i0 = group * 2
    own_piece = lax.div(i0, piece_blocks)
    x_at, y_at, z_at = lax.rem(group, x_size), lax.div(group, x_size), lax.rem(me, 8)
    core_peer = n + 1 - 2 * lax.rem(n, 2)
    row_peer = lax.rem(n + 2, 4)
    far_peer = 3 - n

    def dest_of(e):
        h = lax.rem(e + half, 2)
        return 4 * e + m + h * (3 - 2 * m), i0 + h

    def source_of(i):
        h = lax.rem(i, 2)
        return lax.div(i, 2) * 8 + lax.rem(half + h, 2) * 4 + m + h * (3 - 2 * m)

    def remote(src, dst, ssem, rsem, wide, narrow):
        return pltpu.make_async_remote_copy(
            src_ref=src, dst_ref=dst, send_sem=ssem, recv_sem=rsem,
            device_id={"wide": wide, "narrow": narrow}, device_id_type=pl.DeviceIdType.MESH,
        )

    def await_bytes(ref, sem):
        pltpu.make_async_copy(ref, ref, sem).wait()

    owned = [
        pltpu.make_async_copy(ref, wall.at[m, k], l_sem.at[2 + k])
        for k, ref in enumerate((wg, wu, wd))
    ]
    for copy in owned:
        copy.start()

    barrier = pltpu.get_barrier_semaphore()

    def signal(wide, narrow):
        pl.semaphore_signal(
            barrier, inc=1, device_id={"wide": wide, "narrow": narrow},
            device_id_type=pl.DeviceIdType.MESH,
        )

    for turn in range(1, 8):
        signal(8 * group + lax.rem(z_at + turn, 8), n)
    for peer in (core_peer, row_peer, far_peer):
        signal(me, peer)
    along_x = [
        (y_at * x_size + lax.rem(x_at + turn, x_size)) * 8 + z_at for turn in range(1, x_size)
    ]
    along_y = [
        (lax.rem(y_at + turn, y_size) * x_size + x_at) * 8 + z_at for turn in range(1, y_size)
    ]
    for peer in (*along_x, *along_y):
        signal(peer, n)

    def piece(ref, f, q):
        low, size = chunks[f]
        return ref.at[q, :, pl.ds(low, size)]

    def ag_right(f, q):
        return remote(
            piece(wall, f, q), piece(wall, f, q), ag_send.at[0, f, q], ag_recv.at[f, q], me + 1, n
        )

    def ag_left(f, q):
        return remote(
            piece(wall, f, q), piece(wall, f, q), ag_send.at[1, f, q], ag_recv.at[f, q], me - 1, n
        )

    def ag_own(f):
        @pl.when(m < 3)
        def _():
            ag_right(f, m).start()

        @pl.when(m > 0)
        def _():
            ag_left(f, m).start()

    def ag_await(f, q):
        await_bytes(piece(wall, f, q), ag_recv.at[f, q])

    def ag_late(fs):
        for f in fs:
            @pl.when(m == 0)
            def _():
                ag_right(f, 0).start()

            @pl.when(m == 3)
            def _():
                ag_left(f, 3).start()

    middle = (
        (1, 0, ag_right, 2, 3, ag_left),
        (2, 3, ag_left, 1, 0, ag_right),
    )

    def near_fill(f):
        for own, near, send, _, _, _ in middle:
            @pl.when(m == own)
            def _():
                ag_await(f, near)
                send(f, near).start()
                if f + 2 < nf:
                    send(f + 2, own).start()

    def back_fill(f):
        for own, _, _, near, far, send in middle:
            @pl.when(m == own)
            def _():
                for q in (near, far):
                    ag_await(f, q)
                    send(f, q).start()
                if f + 2 < nf:
                    send(f + 2, own).start()

    def end_fill(f):
        for own, others in ((0, (1, 2, 3)), (3, (2, 1, 0))):
            @pl.when(m == own)
            def _():
                for q in others:
                    ag_await(f, q)

    def pass_on(sem, peers):
        for peer in peers:
            pl.semaphore_signal(
                sem, inc=1, device_id={"wide": peer, "narrow": n},
                device_id_type=pl.DeviceIdType.MESH,
            )

    pl.semaphore_wait(barrier, 10 + len(along_x) + len(along_y))
    pass_on(enter.at[0], along_x)
    for copy in owned:
        copy.wait()
    ag_own(0)
    ag_own(1)
    if along_x:
        pl.semaphore_wait(enter.at[0], len(along_x))
    pass_on(enter.at[1], along_y)

    def iota(shape, axis):
        return lax.broadcasted_iota(jnp.int32, shape, axis).astype(F32)

    slots = experts * CAP
    row_i, col_i = iota((toks, toks), 0), iota((toks, toks), 1)
    diag = row_i == col_i
    idf = ids[...].astype(F32)
    onehot = jnp.where(iota((experts, toks), 0) == idf, 1.0, 0.0)
    before = jnp.where(row_i < col_i, 1.0, 0.0).astype(BF16)
    rank = jnp.sum(dot(onehot.astype(BF16), before) * onehot, axis=0, keepdims=True)
    slot_row = idf * CAP + rank
    slot = jnp.sum(jnp.where(diag, slot_row, 0.0), axis=1, keepdims=True)
    place[...] = jnp.where(iota((toks, slots), 1) == slot, 1.0, 0.0).astype(BF16)
    prob_col = jnp.sum(jnp.where(diag, prob[...], 0.0), axis=1, keepdims=True)
    probs[...] = jnp.broadcast_to(prob_col, (toks, quarter))
    columns = pl.ds(pl.multiple_of(n * quarter, quarter), quarter)
    pick = jnp.where(iota((slots, toks), 0) == slot_row, 1.0, 0.0).astype(BF16)
    scaled = (prob_col * cot[:, columns].astype(F32)).astype(BF16)
    sendbuf[:, :quarter] = dot(pick, tok[:, columns]).astype(BF16)
    sendbuf[:, quarter:] = dot(pick, scaled).astype(BF16)

    if along_y:
        pl.semaphore_wait(enter.at[1], len(along_y))

    def rows_at(i):
        return pl.ds(pl.multiple_of(i * CAP, CAP), CAP)

    def rows_of(p):
        return pl.ds(pl.multiple_of(p * piece_rows, piece_rows), piece_rows)

    def piece_at(turn):
        return lax.rem(own_piece + turn, pieces)

    pltpu.make_async_copy(
        sendbuf.at[rows_at(e0)], x4.at[n, rows_at(i0)], a_recv.at[own_piece]
    ).start()

    def send_block(j):
        e = lax.rem(e0 + j, experts)
        wide, block = dest_of(e)
        remote(
            sendbuf.at[rows_at(e)], x4.at[n, rows_at(block)], a_send, a_recv.at[own_piece], wide, n
        ).start()

    pl.loop(experts // 2, experts)(send_block)
    pl.loop(1, experts // 2)(send_block)

    def x_copy(k, slot, turn, peer):
        part = x4.at[slot, rows_of(piece_at(turn))]
        return remote(
            part, part, n_send.at[k, piece_at(turn)], n_recv.at[slot, piece_at(turn)], me, peer
        )

    def x_await(slot, turn):
        p = piece_at(turn)
        await_bytes(x4.at[slot, rows_of(p)], n_recv.at[slot, p])

    x_sent = []

    def x_share(turn):
        await_bytes(x4.at[n, rows_of(piece_at(turn))], a_recv.at[piece_at(turn)])
        for k, peer in ((1, row_peer), (0, core_peer)):
            copy = x_copy(k, n, turn, peer)
            copy.start()
            x_sent.append(copy)

    def x_relay(turn):
        x_await(row_peer, turn)
        copy = x_copy(2, row_peer, turn, core_peer)
        copy.start()
        x_sent.append(copy)

    out_acc[...] = jnp.zeros_like(out_acc)
    in_acc[...] = jnp.zeros_like(in_acc)
    near_fill(0)
    back_fill(0)
    for turn in turns:
        x_share(turn)
    ag_late(range(2, nf))
    near_fill(1)
    back_fill(1)
    for turn in turns:
        x_relay(turn)
    near_fill(2)
    near_fill(3)
    for slot in (core_peer, far_peer):
        for turn in turns:
            x_await(slot, turn)

    def rs_right(f, q):
        return remote(
            piece(stage, f, q), piece(r_right, f, q), rs_send.at[f, q], rs_recv.at[0, f, q], me + 1, n
        )

    def rs_left(f, q):
        return remote(
            piece(stage, f, q), piece(r_left, f, q), rs_send.at[f, q], rs_recv.at[1, f, q], me - 1, n
        )

    def rs_first(f, q):
        low, size = chunks[f]
        part = pl.ds(low, size)
        for own, send in ((0, rs_right), (3, rs_left)):
            @pl.when((m == own) & (q != own))
            def _():
                stage[q, :, part] = gloc[q, :, part].astype(BF16)
                send(f, q).start()

    def relay(f, source, k, q, send):
        low, size = chunks[f]
        part = pl.ds(low, size)
        await_bytes(piece(source, f, q), rs_recv.at[k, f, q])
        stage[q, :, part] = (gloc[q, :, part] + source[q, :, part].astype(F32)).astype(BF16)
        send(f, q).start()

    def relay_a(f, k):
        @pl.when(m == 1)
        def _():
            relay(f, r_right, 0, 3 - k, rs_right)

        @pl.when(m == 2)
        def _():
            relay(f, r_left, 1, k, rs_left)

    def relay_b(f):
        @pl.when(m == 1)
        def _():
            relay(f, r_left, 1, 0, rs_left)

        @pl.when(m == 2)
        def _():
            relay(f, r_right, 0, 3, rs_right)

    def both(q, part):
        return jnp.concatenate([out_acc[q, part], in_acc[q, part]], axis=1)

    back_turns = (2, 1, 3, 0) if pieces == 4 else turns
    t1, t2 = {}, {}

    def share_on_chip(k, q):
        for turn in back_turns:
            p = piece_at(turn)
            part = rows_of(p)
            t1s[k, part] = both(q, part).astype(BF16)
            t1[k, turn] = remote(
                t1s.at[k, part], t1r.at[k, part], t1_send.at[k, p], t1_recv.at[k, p], me, core_peer
            )
            t1[k, turn].start()

    step_rows = min(64, rows)
    eye = jnp.where(iota((256, 256), 0) == iota((256, 256), 1), 1.0, 0.0).astype(BF16)

    for f, (low, size) in enumerate(chunks):
        end_fill(f)
        units = pl.ds(low, size)
        for k, first in ((0, 0), (1, 0), (2, quarter)):
            total = dot_t(x4[0, :, first : first + quarter], wall[0, k, units])
            for q in range(1, 4):
                total += dot_t(x4[q, :, first : first + quarter], wall[q, k, units])
            pre[k, :, :size] = total

        @pl.loop(0, rows // step_rows)
        def _(r):
            part = pl.ds(pl.multiple_of(r * step_rows, step_rows), step_rows)
            gate, up, d_hidden = pre[0, part, :size], pre[1, part, :size], pre[2, part, :size]
            sigma = jax.nn.sigmoid(gate)
            active = gate * sigma
            d_gate = d_hidden * up * sigma * (1.0 + gate * (1.0 - sigma))
            act3[0, part, :size] = (active * up).astype(BF16)
            act3[1, part, :size] = d_gate.astype(BF16)
            act3[2, part, :size] = (d_hidden * active).astype(BF16)

        def transpose():
            for k in range(3):
                act_t[k, :size] = dot_t(eye[:size, :size], act3[k, :, :size]).astype(BF16)

        def gradients():
            @pl.loop(0, 4)
            def _(step):
                q = step + lax.div(3 - m, 2) * (3 - 2 * step)
                gloc[q, 0, units] = dot(act_t[1, :size], x4[q, :, :quarter])
                gloc[q, 1, units] = dot(act_t[2, :size], x4[q, :, :quarter])
                gloc[q, 2, units] = dot(act_t[0, :size], x4[q, :, quarter:])
                rs_first(f, q)

        def row_sum(q):
            out_acc[q] += dot(act3[0, :, :size], wall[q, 2, units])
            in_acc[q] += dot(act3[1, :, :size], wall[q, 0, units]) + dot(
                act3[2, :, :size], wall[q, 1, units]
            )

        if f < nf - 1:
            transpose()
            gradients()
            pl.loop(0, 4)(row_sum)
        else:
            for k, q in ((1, far_peer), (0, core_peer)):
                row_sum(q)
                share_on_chip(k, q)
            row_sum(row_peer)
            row_sum(n)
            transpose()
            gradients()
        if f < 2:
            relay_a(f, 0)
            back_fill(f + 2)
            relay_a(f, 1)
        if f == 2:
            relay_b(0)

    for turn in back_turns:
        p = piece_at(turn)
        part = rows_of(p)
        t1[1, turn].wait_recv()
        t2s[part] = (both(row_peer, part) + t1r[1, part].astype(F32)).astype(BF16)
        t2[turn] = remote(t2s.at[part], t2r.at[part], t2_send.at[p], t2_recv.at[p], me, row_peer)
        t2[turn].start()

    def send_back(turn):
        p = piece_at(turn)
        part = rows_of(p)
        t1[0, turn].wait_recv()
        t2[turn].wait_recv()
        total = both(n, part) + t1r[0, part].astype(F32) + t2r[part].astype(F32)
        fo[part] = total.astype(BF16)

        @pl.loop(0, piece_blocks)
        def _(j):
            i = p * piece_blocks + j

            @pl.when(i == i0)
            def _():
                pltpu.make_async_copy(fo.at[rows_at(i)], back.at[rows_at(e0)], b_recv).start()

            @pl.when(i != i0)
            def _():
                remote(
                    fo.at[rows_at(i)], back.at[rows_at(e0)], b_send, b_recv, source_of(i), n
                ).start()

    relay_a(2, 0)
    relay_b(1)
    for turn in back_turns:
        if turn == back_turns[-1]:
            relay_b(2)
            relay_a(3, 0)
        send_back(turn)
        if turn == back_turns[0]:
            relay_a(2, 1)
    relay_a(3, 1)
    relay_b(nf - 1)

    written = []

    def finish(f):
        low, size = chunks[f]
        part = pl.ds(low, size)

        @pl.when(m > 0)
        def _():
            await_bytes(piece(r_right, f, m), rs_recv.at[0, f, m])
            gloc[m, :, part] += r_right[m, :, part].astype(F32)

        @pl.when(m < 3)
        def _():
            await_bytes(piece(r_left, f, m), rs_recv.at[1, f, m])
            gloc[m, :, part] += r_left[m, :, part].astype(F32)

        copy = pltpu.make_async_copy(gloc.at[m, :, part], o_weights.at[:, part], o_sem.at[f])
        copy.start()
        written.append(copy)

    for f in range(nf - 1):
        finish(f)

    await_bytes(back, b_recv)
    ffn = dot(place[...], back[:, :quarter])
    rows_out[0] = (probs[...] * ffn).astype(BF16)
    rows_out[1] = dot(place[...], back[:, quarter:]).astype(BF16)
    copy = pltpu.make_async_copy(rows_out, o_rows, l_sem.at[0])
    copy.start()
    written.append(copy)
    part_col = jnp.sum(ffn * cot[:, columns].astype(F32), axis=1, keepdims=True)
    part_row = jnp.sum(jnp.where(diag, part_col, 0.0), axis=0, keepdims=True)
    parts[n] = jnp.broadcast_to(part_row, parts.shape[1:])
    sent = []
    for k, peer in enumerate((core_peer, row_peer, far_peer)):
        copy = remote(parts.at[n], parts.at[n], p_send.at[k], p_recv.at[n], me, peer)
        copy.start()
        sent.append(copy)
    for peer in (core_peer, row_peer, far_peer):
        await_bytes(parts.at[peer], p_recv.at[peer])
    prob_out[...] = (parts[0] + parts[1] + parts[2] + parts[3])[:1]
    copy = pltpu.make_async_copy(prob_out, o_prob, l_sem.at[1])
    copy.start()
    written.append(copy)
    finish(nf - 1)

    for copy in (*sent, *x_sent, *t1.values(), *t2.values()):
        copy.wait_send()
    for copy in written:
        copy.wait()
    await_bytes(sendbuf.at[pl.ds(0, slots - CAP)], a_send)
    await_bytes(fo.at[pl.ds(0, rows - CAP)], b_send)

    for f in range(nf):
        for q in range(4):
            @pl.when(m != q)
            def _():
                await_bytes(piece(stage, f, q), rs_send.at[f, q])

            @pl.when((m < 3) & (m >= q))
            def _():
                await_bytes(piece(wall, f, q), ag_send.at[0, f, q])

            @pl.when((m > 0) & (m <= q))
            def _():
                await_bytes(piece(wall, f, q), ag_send.at[1, f, q])


def shards(wide, tokens, cotangent, expert_ids, route_prob, gate_weight, up_weight, down_weight):
    toks, width = tokens.shape
    quarter, ff = gate_weight.shape
    experts = wide // 4
    slots = experts * CAP
    rows = wide // 4 * CAP
    nf = len(cuts(ff))
    chunk = cuts(ff)[0][1]
    pieces = piece_count(experts)
    any_spec = pl.BlockSpec(memory_space=pl.ANY)
    vmem, dma = pltpu.VMEM, pltpu.SemaphoreType.DMA
    spec = pl.BlockSpec(memory_space=pltpu.VMEM)
    two = 2 * quarter
    row_outs, prob_out, grads = pl.pallas_call(
        kernel,
        out_shape=(
            jax.ShapeDtypeStruct((2, toks, quarter), BF16),
            jax.ShapeDtypeStruct((1, toks), F32),
            jax.ShapeDtypeStruct((3, ff, quarter), F32),
        ),
        in_specs=[spec] * 4 + [any_spec] * 3,
        out_specs=(any_spec, any_spec, any_spec),
        scratch_shapes=[
            vmem((4, 3, ff, quarter), BF16),
            vmem((slots, two), BF16),
            vmem((4, rows, two), BF16),
            vmem((3, chunk, rows), BF16),
            vmem((3, rows, chunk), F32),
            vmem((3, rows, chunk), BF16),
            vmem((4, rows, quarter), F32),
            vmem((4, rows, quarter), F32),
            vmem((4, 3, ff, quarter), F32),
            vmem((4, 3, ff, quarter), BF16),
            vmem((4, 3, ff, quarter), BF16),
            vmem((4, 3, ff, quarter), BF16),
            vmem((2, rows, two), BF16),
            vmem((2, rows, two), BF16),
            vmem((rows, two), BF16),
            vmem((rows, two), BF16),
            vmem((rows, two), BF16),
            vmem((slots, two), BF16),
            vmem((toks, slots), BF16),
            vmem((toks, quarter), F32),
            vmem((4, 8, toks), F32),
            vmem((2, toks, quarter), BF16),
            vmem((1, toks), F32),
            dma((2, nf, 4)), dma((nf, 4)), dma((nf, 4)), dma((2, nf, 4)),
            dma, dma((pieces,)), dma((5,)), dma((3, pieces)), dma((4, pieces)),
            dma((2, pieces)), dma((2, pieces)), dma((pieces,)), dma((pieces,)),
            dma, dma, dma((3,)), dma((4,)), dma((nf,)), pltpu.SemaphoreType.REGULAR((2,)),
        ],
        compiler_params=pltpu.CompilerParams(
            collective_id=0, has_side_effects=True, vmem_limit_bytes=63000 * 1024
        ),
    )(
        tokens, cotangent, expert_ids.reshape(1, toks), route_prob.reshape(1, toks),
        gate_weight.T, up_weight.T, down_weight.T,
    )
    return row_outs[0], row_outs[1], prob_out.reshape(toks), grads[0].T, grads[1].T, grads[2].T


def solution(mesh):
    in_specs = (
        P("wide", None),
        P("wide", None),
        P("wide", None),
        P("wide"),
        P("wide", "narrow"),
        P("wide", "narrow"),
        P("wide", "narrow"),
    )
    out_specs = (
        P("wide", "narrow"),
        P("wide", "narrow"),
        P("wide"),
        P("wide", "narrow"),
        P("wide", "narrow"),
        P("wide", "narrow"),
    )
    return jax.shard_map(
        functools.partial(shards, mesh.shape["wide"]),
        mesh=mesh, in_specs=in_specs, out_specs=out_specs, check_vma=False,
    )
```
